32 devices in a mesh: row: 8 (over z, y), col: 4 (over x, core).
Axes of the slice: x: 2, y: 2, z: 4, core: 2. Of those that a mesh axis runs over, the one named last changes fastest.
Arguments:
- entries: int32 [32, 16, 128, 128], P('row', 'col'), may hold values from -2 to 2
- tile_cols: int32 [32, 16], P('row', 'col'), may hold values from 0 to 31
- block_now: int32 [32, 16384], P(None, ('col', 'row')), may hold values from 0 to 65520
- block_prev: int32 [32, 16384], P(None, ('col', 'row')), may hold values from 0 to 65520
- block_prev2: int32 [32, 16384], P(None, ('col', 'row')), may hold values from 0 to 65520
- gram_prev: int32 [32, 32], replicated, may hold values from 0 to 65520
- square_prev: int32 [32, 32], replicated, may hold values from 0 to 65520
- inverse_prev: int32 [32, 32], replicated, may hold values from 0 to 65520
- inverse_prev2: int32 [32, 32], replicated, may hold values from 0 to 65520
Outputs:
- next_block: float32 [32, 16384], P(None, ('col', 'row'))
- later_block: float32 [32, 16384], P(None, ('col', 'row'))
The draws below stay inside these ranges and needn't reach their ends.
Inputs may be any that keep to these rules, and one draw needn't show every extreme that they name: `tile_cols`: stored tiles that name the same tile column in one tile row add. `block_prev`: residues. `block_prev2`: residues. `gram_prev`: residues. `square_prev`: residues. `inverse_prev`: residues. `inverse_prev2`: residues.
All inputs are finite; a program needn't handle non-finite values.
Results may differ from the reference program's by a relative error of at most 0.0003.
Values sent between devices are 32-bit elements; how exact they have to be, the bound alone decides.
A program may use at most 64 MiB of HBM per device.

```python
import jax
import jax.numpy as jnp
from jax import lax

BLOCK = 32
TILE = 128
SLOTS = 4
TCOLS = 32
ORDER = 16384
TROWS_ALL = 32
SLOTS_ALL = 16
N_COL = 4


def with_ends(values, key, least, top_value):
    extent = values.shape
    index_at = [jax.random.randint(jax.random.fold_in(key, axis), (), 0, extent[axis]) for axis in range(len(extent))]
    values = values.at[tuple(index_at)].set(least)
    longest = extent.index(max(extent))
    index_at[longest] = (index_at[longest] + 1) % extent[longest]
    return values.at[tuple(index_at)].set(top_value)


def setup_inputs(seed: int = 0) -> dict:
    seeds = jax.random.split(jax.random.key(seed), 10)
    return {
        "entries": with_ends(jax.random.randint(seeds[0], (TROWS_ALL, SLOTS_ALL, TILE, TILE), -2, 3), jax.random.fold_in(seeds[0], 1), -2, 2).astype(jnp.int32),
        "tile_cols": with_ends(jax.random.randint(seeds[1], (TROWS_ALL, SLOTS_ALL), 0, TCOLS), jax.random.fold_in(seeds[1], 1), 0, TCOLS - 1).astype(jnp.int32),
        "block_now": with_ends(jax.random.randint(seeds[2], (BLOCK, ORDER), 0, 65521), jax.random.fold_in(seeds[2], 1), 0, 65520).astype(jnp.int32),
        "block_prev": with_ends(jax.random.randint(seeds[3], (BLOCK, ORDER), 0, 65521), jax.random.fold_in(seeds[3], 1), 0, 65520).astype(jnp.int32),
        "block_prev2": with_ends(jax.random.randint(seeds[4], (BLOCK, ORDER), 0, 65521), jax.random.fold_in(seeds[4], 1), 0, 65520).astype(jnp.int32),
        "gram_prev": with_ends(jax.random.randint(seeds[5], (BLOCK, BLOCK), 0, 65521), jax.random.fold_in(seeds[5], 1), 0, 65520).astype(jnp.int32),
        "square_prev": with_ends(jax.random.randint(seeds[6], (BLOCK, BLOCK), 0, 65521), jax.random.fold_in(seeds[6], 1), 0, 65520).astype(jnp.int32),
        "inverse_prev": with_ends(jax.random.randint(seeds[7], (BLOCK, BLOCK), 0, 65521), jax.random.fold_in(seeds[7], 1), 0, 65520).astype(jnp.int32),
        "inverse_prev2": with_ends(jax.random.randint(seeds[8], (BLOCK, BLOCK), 0, 65521), jax.random.fold_in(seeds[8], 1), 0, 65520).astype(jnp.int32),
    }


modulus = 65521.0


def residue(values):
    return jnp.mod(values, modulus)


def split_digits(values):
    top_part = jnp.floor(values / 256.0)
    return top_part, values - top_part * 256.0


def fold_digits(top_sum, low_sum):
    return residue(residue(residue(top_sum) * 256.0) + residue(low_sum))


def fold_three(upper_part, middle, lower_part):
    return residue(residue(residue(upper_part) * 15.0) + residue(residue(middle) * 256.0) + residue(lower_part))


def mulmod(left_side, right_side):
    top_part, low_part = split_digits(right_side)
    return fold_digits(left_side * top_part, left_side * low_part)


def exact_dot(left_side, right_side):
    return jnp.dot(left_side, right_side, precision=lax.Precision.HIGHEST, preferred_element_type=jnp.float32)


def small_product(left_side, right_side):
    left_top, left_low = split_digits(left_side)
    right_top, right_low = split_digits(right_side)
    return fold_three(exact_dot(left_top, right_top), exact_dot(left_top, right_low) + exact_dot(left_low, right_top), exact_dot(left_low, right_low))


def inverse_scalar(number):
    result = jnp.ones_like(number)
    square = number
    exponent = 65519
    for position in range(16):
        if (exponent >> position) & 1:
            result = mulmod(result, square)
        square = mulmod(square, square)
    return result


def inverse_matrix(matrix):
    matrix_order = matrix.shape[0]
    augmented = jnp.concatenate([matrix, jnp.eye(matrix_order, dtype=matrix.dtype)], axis=1)
    row_numbers = jnp.arange(matrix_order, dtype=jnp.int32)

    def eliminate(column, augmented):
        column = jnp.asarray(column).astype(jnp.int32)
        pivot_column = augmented[:, column]
        usable = (pivot_column != 0.0) & (row_numbers >= column)
        pivot_row_id = jnp.where(jnp.any(usable), jnp.argmax(usable).astype(jnp.int32), column)
        pivot_row = augmented[pivot_row_id]
        current_row = augmented[column]
        swapped = jnp.where((row_numbers == column)[:, None], pivot_row[None, :], jnp.where((row_numbers == pivot_row_id)[:, None], current_row[None, :], augmented))
        scaled = mulmod(pivot_row, inverse_scalar(pivot_row[column]))
        factors = jnp.where(row_numbers == column, 0.0, swapped[:, column])
        reduced = residue(swapped - mulmod(factors[:, None], scaled[None, :]) + modulus)
        return jnp.where((row_numbers == column)[:, None], scaled[None, :], reduced)

    augmented = lax.fori_loop(0, matrix_order, eliminate, augmented)
    return augmented[:, matrix_order:]


def coefficients(gram_now, square_now, inverse_now, inverse_prev, inverse_prev2, gram_old, square_old):
    identity = jnp.eye(gram_now.shape[0], dtype=gram_now.dtype)
    first = residue(identity - small_product(residue(square_now + gram_now), inverse_now) + modulus)
    second = residue(modulus - small_product(gram_now, inverse_prev))
    middle = residue(identity - small_product(inverse_prev, gram_old) + modulus)
    third = residue(modulus - small_product(small_product(residue(square_old + gram_old), middle), inverse_prev2))
    return jnp.concatenate([first, second, third], axis=1)


def combine_blocks(coeffs, stacked):
    coeff_top, coeff_low = split_digits(coeffs)
    stack_top, stack_low = split_digits(stacked)
    left_side = jnp.stack([coeff_top, coeff_low])
    right_side = jnp.stack([stack_top, stack_low])
    products = jnp.einsum('dab,ebn->dean', left_side, right_side, precision=lax.Precision.HIGHEST)
    return fold_three(products[0, 0], products[0, 1] + products[1, 0], products[1, 1])


def gram_whole(first, second):
    column_count = first.shape[1]
    group_width = min(column_count, 128)
    groups = column_count // group_width
    first_digits = jnp.stack(split_digits(first)).reshape(2, first.shape[0], groups, group_width)
    second_digits = jnp.stack(split_digits(second)).reshape(2, second.shape[0], groups, group_width)
    products = jnp.einsum('dagw,ecgw->gdeac', first_digits, second_digits, precision=lax.Precision.HIGHEST)
    per_group = fold_three(products[:, 0, 0], products[:, 0, 1] + products[:, 1, 0], products[:, 1, 1])
    top_part, low_part = split_digits(per_group)
    return fold_digits(jnp.sum(top_part, axis=0), jnp.sum(low_part, axis=0))


def reference(entries, tile_cols, block_now, block_prev, block_prev2, gram_prev, square_prev, inverse_prev, inverse_prev2):
    col_tiles = TCOLS * N_COL
    slot_owner = (jnp.arange(SLOTS * N_COL, dtype=jnp.int32) // SLOTS) * TCOLS
    global_cols = (tile_cols + slot_owner[None, :]).astype(jnp.int32)

    def apply_operator(block):
        top_part, low_part = split_digits(block)
        digits = jnp.concatenate([top_part, low_part], axis=0).reshape(2 * BLOCK, col_tiles, TILE)

        def per_row(running, inputs):
            tile_row, cols_row = inputs
            matrix = tile_row.astype(jnp.float32)
            picked = jnp.take(digits, cols_row, axis=1)
            raw_sums = jnp.einsum('bsk,sjk->bj', picked, matrix, precision=lax.Precision.HIGHEST)
            projected = fold_digits(raw_sums[:BLOCK], raw_sums[BLOCK:])
            proj_top, proj_low = split_digits(projected)
            proj_digits = jnp.concatenate([proj_top, proj_low], axis=0)
            spread = jnp.einsum('bj,sjk->bsk', proj_digits, matrix, precision=lax.Precision.HIGHEST)
            per_slot = fold_digits(spread[:BLOCK], spread[BLOCK:])
            return residue(running.at[:, cols_row, :].add(per_slot)), None

        totals, unused = lax.scan(per_row, jnp.zeros((BLOCK, col_tiles, TILE), jnp.float32), (entries, global_cols))
        return totals.reshape(BLOCK, col_tiles * TILE)

    current = block_now.astype(jnp.float32)
    earlier = block_prev.astype(jnp.float32)
    earliest = block_prev2.astype(jnp.float32)
    gram_old = gram_prev.astype(jnp.float32)
    square_old = square_prev.astype(jnp.float32)
    inverse_old = inverse_prev.astype(jnp.float32)
    inverse_older = inverse_prev2.astype(jnp.float32)
    results = []
    for iteration in range(2):
        applied = apply_operator(current)
        gram_now = gram_whole(current, applied)
        square_now = gram_whole(applied, applied)
        inverse_now = inverse_matrix(gram_now)
        coeffs = coefficients(gram_now, square_now, inverse_now, inverse_old, inverse_older, gram_old, square_old)
        stacked = jnp.concatenate([current, earlier, earliest], axis=0)
        following = residue(applied + combine_blocks(coeffs, stacked))
        results.append(following / modulus)
        earliest, earlier, current = earlier, current, following
        inverse_older, inverse_old = inverse_old, inverse_now
        gram_old, square_old = gram_now, square_now
    return results[0], results[1]
```

```python
import functools

import jax
import jax.numpy as jnp
from jax import lax
from jax.experimental import pallas as pl
from jax.experimental.pallas import tpu as pltpu
from jax.sharding import PartitionSpec as P

modulus = 65521.0
reciprocal = 1.0 / 65521.0
MESH = pl.DeviceIdType.MESH
GATHER, PARTIAL, SCATTER, GRAM, SQUARE_ROW, SQUARE_COL = range(6)


def near(values):
    return values - jnp.floor(values * reciprocal + 0.5) * modulus


def whole(values):
    signed = near(values)
    return jnp.where(signed < 0.0, signed + modulus, signed)


def split(values):
    top = jnp.floor(values * (1.0 / 256.0) + 0.5)
    return top, values - top * 256.0


def digits(values):
    top, low = split(values)
    return jnp.concatenate([top, low], axis=0).astype(jnp.bfloat16)


def fold_two(top, low):
    return near(near(top) * 256.0 + low)


def fold_three(upper, middle, lower):
    return near(near(upper) * 15.0 + near(middle) * 256.0 + near(lower))


def mulmod(left, right):
    top, low = split(right)
    return near(near(left * top) * 256.0 + left * low)


def dot(left, right):
    return jnp.dot(left, right, preferred_element_type=jnp.float32)


def dot_t(left, right):
    return lax.dot_general(
        left, right, (((1,), (1,)), ((), ())), preferred_element_type=jnp.float32
    )


def product_parts(left, right):
    order = left.shape[0]
    left_digits = digits(left)
    right_top, right_low = split(right)
    with_top = dot(left_digits, right_top.astype(jnp.bfloat16))
    with_low = dot(left_digits, right_low.astype(jnp.bfloat16))
    return with_top[:order], with_top[order:] + with_low[:order], with_low[order:]


def small_product(left, right):
    return fold_three(*product_parts(left, right))


def gram_tiles(tiles):
    order = tiles[0].shape[0]
    total = None
    for tile in tiles:
        both = digits(tile)
        term = dot_t(both, both)
        total = term if total is None else total + term
    return fold_three(
        total[:order, :order],
        total[:order, order:] + total[order:, :order],
        total[order:, order:],
    )


def power_inverse(number):
    result = None
    square = number
    for position in range(16):
        if 65519 >> position & 1:
            result = square if result is None else mulmod(result, square)
        if position < 15:
            square = mulmod(square, square)
    return result


def identity_of(order):
    rows = lax.broadcasted_iota(jnp.int32, (order, order), 0)
    lanes = lax.broadcasted_iota(jnp.int32, (order, order), 1)
    return jnp.where(rows == lanes, 1.0, 0.0).astype(jnp.float32)


def inverse_of(matrix):
    order = matrix.shape[0]
    work = jnp.concatenate([matrix, identity_of(order)], axis=1)
    rows = lax.broadcasted_iota(jnp.int32, (order, 1), 0)
    for column in range(order):
        entry = work[:, column : column + 1]
        usable = (entry != 0.0) & (rows >= column)
        first = jnp.min(jnp.where(usable, rows, order), axis=0, keepdims=True)
        chosen = rows == jnp.where(first == order, column, first)
        pivot_row = jnp.sum(jnp.where(chosen, work, 0.0), axis=0, keepdims=True)
        pivot = jnp.sum(jnp.where(chosen, entry, 0.0), axis=0, keepdims=True)
        swapped = jnp.where(chosen, work[column : column + 1, :], work)
        factor = jnp.where(chosen, entry[column : column + 1, :], entry)
        pivot_row = jnp.where(pivot == 0.0, 0.0, pivot_row)
        pivot = jnp.where(pivot == 0.0, 1.0, pivot)
        pivot_top, pivot_low = split(pivot)
        factor_top, factor_low = split(factor)
        upper = near(pivot_top * swapped - factor_top * pivot_row)
        reduced = near(upper * 256.0 + (pivot_low * swapped - factor_low * pivot_row))
        work = jnp.where(rows == column, pivot_row, reduced)
    left = work[:, :order]
    diagonal = jnp.sum(left * identity_of(order), axis=1, keepdims=True)
    return mulmod(work[:, order:], power_inverse(diagonal))


def kernel(
    n_row, n_col, index_ref, entries_ref, now_ref, prev_ref, prev2_ref,
    gram_ref, square_ref, inverse_ref, inverse2_ref, next_ref, later_ref,
    tile16, full_a, full_b, partial, spread, running, outgoing, incoming,
    gram_buf, square_row, square_col, send_sem, recv_sem,
):
    my_row = lax.axis_index("row")
    my_col = lax.axis_index("col")
    tile_rows, slots, size = entries_ref.shape[:3]
    stored = tile_rows * slots
    order = now_ref.shape[0]
    share = now_ref.shape[1] // size
    col_tiles = n_row * share
    started = []

    def row_peer(k):
        return lax.rem(my_row + k, n_row)

    def col_peer(k):
        return lax.rem(my_col + k, n_col)

    barrier = pltpu.get_barrier_semaphore()
    for k in range(1, n_row):
        pl.semaphore_signal(barrier, inc=1, device_id=(row_peer(k), my_col), device_id_type=MESH)
    for k in range(1, n_col):
        pl.semaphore_signal(barrier, inc=1, device_id=(my_row, col_peer(k)), device_id_type=MESH)

    def send(step, phase, k, source, target, device):
        copy = pltpu.make_async_remote_copy(
            src_ref=source, dst_ref=target,
            send_sem=send_sem.at[step, phase, k], recv_sem=recv_sem.at[step, phase, k],
            device_id=device, device_id_type=MESH,
        )
        copy.start()
        started.append(copy)
        return copy

    def tiles_of(values):
        return [values[:, t * size : (t + 1) * size] for t in range(share)]

    def load(ref):
        return tiles_of(near(ref[...].astype(jnp.float32)))

    current, earlier, earliest = load(now_ref), load(prev_ref), load(prev2_ref)
    gram_old = near(gram_ref[...].astype(jnp.float32))
    square_old = near(square_ref[...].astype(jnp.float32))
    inverse_old = near(inverse_ref[...].astype(jnp.float32))
    inverse_older = near(inverse2_ref[...].astype(jnp.float32))
    identity = identity_of(order)
    fulls = (full_a, full_b)
    for t in range(share):
        full_a[my_row * share + t] = current[t]
    pl.semaphore_wait(barrier, n_row + n_col - 2)

    for step in range(2):
        full = fulls[step]
        mine = full.at[pl.ds(my_row * share, share)]
        gathers = [
            send(step, GATHER, k, mine, mine, (row_peer(k), my_col)) for k in range(1, n_row)
        ]
        if step == 0:
            for i in range(stored):
                tile16[i] = entries_ref[i // slots, i % slots].astype(jnp.float32).astype(jnp.bfloat16)
        middle = near(identity - small_product(inverse_old, gram_old))
        third = -small_product(
            small_product(near(square_old + gram_old), middle), inverse_older
        )
        for copy in gathers:
            copy.wait_recv()

        for r in range(tile_rows):
            total = None
            for s in range(slots):
                picked = full[index_ref[r * slots + s]]
                term = dot_t(digits(picked), tile16[r * slots + s])
                total = term if total is None else total + term
            partial[step, my_col, r] = fold_two(total[:order], total[order:])
        own = partial.at[step, my_col]
        sends = [
            send(step, PARTIAL, k, own, own, (my_row, col_peer(k))) for k in range(1, n_col)
        ]
        for copy in sends:
            copy.wait_recv()
        projected = []
        for r in range(tile_rows):
            total = partial[step, 0, r]
            for c in range(1, n_col):
                total = total + partial[step, c, r]
            projected.append(near(total))

        gram_buf[step, my_row] = gram_tiles(projected)
        own = gram_buf.at[step, my_row]
        grams = [send(step, GRAM, k, own, own, (row_peer(k), my_col)) for k in range(1, n_row)]

        for r in range(tile_rows):
            both = digits(projected[r])
            for s in range(slots):
                spread[r * slots + s] = dot(both, tile16[r * slots + s])
        total = jnp.zeros((2 * order, size), jnp.float32)
        running[0] = total
        for i in range(stored):
            total = total + spread[index_ref[stored + i]]
            running[i + 1] = total
        scatters = []
        for k in list(range(1, n_row)) + [0]:
            peer = row_peer(k)
            for t in range(share):
                tile = peer * share + t
                begin = index_ref[2 * stored + tile]
                end = index_ref[2 * stored + col_tiles + tile]
                summed = running[end] - running[begin]
                outgoing[step, tile] = fold_two(summed[:order], summed[order:])
            if k:
                scatters.append(
                    send(
                        step, SCATTER, k, outgoing.at[step, pl.ds(peer * share, share)],
                        incoming.at[step, my_row], (peer, my_col),
                    )
                )

        for copy in grams:
            copy.wait_recv()
        total = gram_buf[step, 0]
        for r in range(1, n_row):
            total = total + gram_buf[step, r]
        gram_now = near(total)
        inverse_now = inverse_of(gram_now)
        second = -small_product(gram_now, inverse_old)
        parts = []
        for t in range(share):
            one = product_parts(second, earlier[t])
            two = product_parts(third, earliest[t])
            parts.append([a + b for a, b in zip(one, two)])

        for copy in scatters:
            copy.wait_recv()
        applied = []
        for t in range(share):
            total = outgoing[step, my_row * share + t]
            for k in range(1, n_row):
                total = total + incoming[step, row_peer(k), t]
            applied.append(near(total))

        square_row[step, my_row] = gram_tiles(applied)
        own = square_row.at[step, my_row]
        sends = [
            send(step, SQUARE_ROW, k, own, own, (row_peer(k), my_col)) for k in range(1, n_row)
        ]
        for copy in sends:
            copy.wait_recv()
        total = square_row[step, 0]
        for r in range(1, n_row):
            total = total + square_row[step, r]
        square_col[step, my_col] = near(total)
        own = square_col.at[step, my_col]
        sends = [
            send(step, SQUARE_COL, k, own, own, (my_row, col_peer(k))) for k in range(1, n_col)
        ]
        for copy in sends:
            copy.wait_recv()
        total = square_col[step, 0]
        for c in range(1, n_col):
            total = total + square_col[step, c]
        square_now = near(total)

        first = near(identity - small_product(near(square_now + gram_now), inverse_now))
        following = []
        for t in range(share):
            upper, mid, lower = [
                a + b for a, b in zip(product_parts(first, current[t]), parts[t])
            ]
            following.append(
                whole(applied[t] + near(upper) * 15.0 + near(mid) * 256.0 + lower)
            )
        out = (next_ref, later_ref)[step]
        if step == 0:
            for t in range(share):
                full_b[my_row * share + t] = near(following[t])
        for t in range(share):
            out[:, t * size : (t + 1) * size] = following[t] / modulus
        earliest, earlier, current = earlier, current, [near(f) for f in following]
        inverse_older, inverse_old = inverse_old, inverse_now
        gram_old, square_old = gram_now, square_now

    for copy in started:
        copy.wait_send()


def body(
    n_row, n_col, entries, tile_cols, block_now, block_prev, block_prev2,
    gram_prev, square_prev, inverse_prev, inverse_prev2,
):
    tile_rows, slots, size = entries.shape[:3]
    order, width = block_now.shape
    share = width // size
    col_tiles = n_row * share
    stored = tile_rows * slots
    assert tile_rows <= 4 and share <= 4

    cols = tile_cols.reshape(-1)
    places = jnp.arange(stored, dtype=jnp.int32)
    ahead = (cols[None, :] < cols[:, None]) | (
        (cols[None, :] == cols[:, None]) & (places[None, :] < places[:, None])
    )
    rank = jnp.sum(ahead.astype(jnp.int32), axis=1)
    ordered = jnp.sum(jnp.where(rank[None, :] == places[:, None], places[None, :], 0), axis=1)
    tiles = jnp.arange(col_tiles, dtype=jnp.int32)
    begin = jnp.sum((cols[None, :] < tiles[:, None]).astype(jnp.int32), axis=1)
    end = jnp.sum((cols[None, :] <= tiles[:, None]).astype(jnp.int32), axis=1)
    index = jnp.concatenate([cols, ordered, begin, end])

    peers = max(n_row, n_col)
    f32 = jnp.float32
    vmem = pl.BlockSpec(memory_space=pltpu.VMEM)
    return pl.pallas_call(
        functools.partial(kernel, n_row, n_col),
        out_shape=(jax.ShapeDtypeStruct((order, width), f32),) * 2,
        in_specs=[pl.BlockSpec(memory_space=pltpu.SMEM)] + [vmem] * 8,
        out_specs=(vmem, vmem),
        scratch_shapes=[
            pltpu.VMEM((stored, size, size), jnp.bfloat16),
            pltpu.VMEM((col_tiles, order, size), f32),
            pltpu.VMEM((col_tiles, order, size), f32),
            pltpu.VMEM((2, n_col, tile_rows, order, size), f32),
            pltpu.VMEM((stored, 2 * order, size), f32),
            pltpu.VMEM((stored + 1, 2 * order, size), f32),
            pltpu.VMEM((2, col_tiles, order, size), f32),
            pltpu.VMEM((2, n_row, share, order, size), f32),
            pltpu.VMEM((2, n_row, order, order), f32),
            pltpu.VMEM((2, n_row, order, order), f32),
            pltpu.VMEM((2, n_col, order, order), f32),
            pltpu.SemaphoreType.DMA((2, 6, peers)),
            pltpu.SemaphoreType.DMA((2, 6, peers)),
        ],
        compiler_params=pltpu.CompilerParams(collective_id=0, has_side_effects=True),
    )(
        index, entries, block_now, block_prev, block_prev2,
        gram_prev, square_prev, inverse_prev, inverse_prev2,
    )


def solution(mesh):
    placed = (
        P("row", "col", None, None),
        P("row", "col"),
        P(None, ("col", "row")),
        P(None, ("col", "row")),
        P(None, ("col", "row")),
        P(),
        P(),
        P(),
        P(),
    )
    return jax.shard_map(
        functools.partial(body, mesh.shape["row"], mesh.shape["col"]),
        mesh=mesh,
        in_specs=placed,
        out_specs=(P(None, ("col", "row")), P(None, ("col", "row"))),
        check_vma=False,
    )
```

```python
import functools

import jax
import jax.numpy as jnp
from jax import lax
from jax.experimental import pallas as pl
from jax.experimental.pallas import tpu as pltpu
from jax.sharding import PartitionSpec as P

modulus = 65521.0
reciprocal = 1.0 / 65521.0
MESH = pl.DeviceIdType.MESH
GATHER, PARTIAL, SCATTER, GRAM, SQUARE_ROW, SQUARE_COL = range(6)


def near(values):
    return values - jnp.floor(values * reciprocal + 0.5) * modulus


def whole(values):
    signed = near(values)
    return jnp.where(signed < 0.0, signed + modulus, signed)


def split(values):
    top = jnp.floor(values * (1.0 / 256.0) + 0.5)
    return top, values - top * 256.0


def digits(values):
    top, low = split(values)
    return jnp.concatenate([top, low], axis=0).astype(jnp.bfloat16)


def fold_two(top, low):
    return near(near(top) * 256.0 + low)


def fold_three(upper, middle, lower):
    return near(near(upper) * 15.0 + near(middle) * 256.0 + near(lower))


def mulmod(left, right):
    top, low = split(right)
    return near(near(left * top) * 256.0 + left * low)


def dot(left, right):
    return jnp.dot(left, right, preferred_element_type=jnp.float32)


def dot_t(left, right):
    return lax.dot_general(
        left, right, (((1,), (1,)), ((), ())), preferred_element_type=jnp.float32
    )


def product_parts(left, right):
    order = left.shape[0]
    left_digits = digits(left)
    right_top, right_low = split(right)
    with_top = dot(left_digits, right_top.astype(jnp.bfloat16))
    with_low = dot(left_digits, right_low.astype(jnp.bfloat16))
    return with_top[:order], with_top[order:] + with_low[:order], with_low[order:]


def small_product(left, right):
    return fold_three(*product_parts(left, right))


def gram_tiles(tiles):
    order = tiles[0].shape[0]
    total = None
    for tile in tiles:
        both = digits(tile)
        term = dot_t(both, both)
        total = term if total is None else total + term
    return fold_three(
        total[:order, :order],
        total[:order, order:] + total[order:, :order],
        total[order:, order:],
    )


def power_inverse(number):
    result = None
    square = number
    for position in range(16):
        if 65519 >> position & 1:
            result = square if result is None else mulmod(result, square)
        if position < 15:
            square = mulmod(square, square)
    return result


def identity_of(order):
    rows = lax.broadcasted_iota(jnp.int32, (order, order), 0)
    lanes = lax.broadcasted_iota(jnp.int32, (order, order), 1)
    return jnp.where(rows == lanes, 1.0, 0.0).astype(jnp.float32)


def inverse_of(matrix):
    order = matrix.shape[0]
    work = jnp.concatenate([matrix, identity_of(order)], axis=1)
    rows = lax.broadcasted_iota(jnp.int32, (order, 1), 0)
    for column in range(order):
        entry = work[:, column : column + 1]
        usable = (entry != 0.0) & (rows >= column)
        first = jnp.min(jnp.where(usable, rows, order), axis=0, keepdims=True)
        chosen = rows == jnp.where(first == order, column, first)
        pivot_row = jnp.sum(jnp.where(chosen, work, 0.0), axis=0, keepdims=True)
        pivot = jnp.sum(jnp.where(chosen, entry, 0.0), axis=0, keepdims=True)
        swapped = jnp.where(chosen, work[column : column + 1, :], work)
        factor = jnp.where(chosen, entry[column : column + 1, :], entry)
        pivot_row = jnp.where(pivot == 0.0, 0.0, pivot_row)
        pivot = jnp.where(pivot == 0.0, 1.0, pivot)
        pivot_top, pivot_low = split(pivot)
        factor_top, factor_low = split(factor)
        upper = near(pivot_top * swapped - factor_top * pivot_row)
        reduced = near(upper * 256.0 + (pivot_low * swapped - factor_low * pivot_row))
        work = jnp.where(rows == column, pivot_row, reduced)
    left = work[:, :order]
    diagonal = jnp.sum(left * identity_of(order), axis=1, keepdims=True)
    return mulmod(work[:, order:], power_inverse(diagonal))


def pack(values):
    rows = values.shape[0] // 4
    return jnp.concatenate([values[g * rows : (g + 1) * rows] for g in range(4)], axis=1)


def unpack(values):
    width = values.shape[1] // 4
    return jnp.concatenate([values[:, g * width : (g + 1) * width] for g in range(4)], axis=0)


def flipped(place, mask, count):
    assert count & (count - 1) == 0
    bit = 1
    moved = place
    while bit < count:
        if mask & bit:
            moved = moved + bit - 2 * bit * lax.rem(place // bit, 2)
        bit *= 2
    return moved


def kernel(
    n_row, n_col, cols_ref, order_ref, begin_ref, end_ref,
    entries_ref, now_ref, prev_ref, prev2_ref,
    gram_ref, square_ref, inverse_ref, inverse2_ref, next_ref, later_ref,
    tile16, full_a, full_b, partial, spread, running, outgoing, incoming,
    gram_buf, square_row, square_col, send_sem, recv_sem,
):
    my_row = lax.axis_index("row")
    my_col = lax.axis_index("col")
    tile_rows, slots, size = entries_ref.shape[:3]
    stored = tile_rows * slots
    order = now_ref.shape[0]
    share = now_ref.shape[1] // size
    half = n_row // 2
    started = []

    def row_peer(m):
        return flipped(my_row, m, n_row)

    def col_peer(m):
        return flipped(my_col, m, n_col)

    barrier = pltpu.get_barrier_semaphore()
    for m in range(1, n_row):
        pl.semaphore_signal(barrier, inc=1, device_id=(row_peer(m), my_col), device_id_type=MESH)
    for m in range(1, n_col):
        pl.semaphore_signal(barrier, inc=1, device_id=(my_row, col_peer(m)), device_id_type=MESH)

    def send(step, phase, k, source, target, device):
        copy = pltpu.make_async_remote_copy(
            src_ref=source, dst_ref=target,
            send_sem=send_sem.at[step, phase, k], recv_sem=recv_sem.at[step, phase, k],
            device_id=device, device_id_type=MESH,
        )
        copy.start()
        started.append(copy)
        return copy

    def tiles_of(values):
        return [values[:, t * size : (t + 1) * size] for t in range(share)]

    def load(ref):
        return tiles_of(near(ref[...].astype(jnp.float32)))

    def block(full, row):
        return full.at[pl.ds(row * share, share)]

    current, earlier, earliest = load(now_ref), load(prev_ref), load(prev2_ref)
    gram_old = near(gram_ref[...].astype(jnp.float32))
    square_old = near(square_ref[...].astype(jnp.float32))
    inverse_old = near(inverse_ref[...].astype(jnp.float32))
    inverse_older = near(inverse2_ref[...].astype(jnp.float32))
    identity = identity_of(order)
    for t in range(share):
        full_a[my_row * share + t] = current[t]
    pl.semaphore_wait(barrier, n_row + n_col - 2)

    def gather_start(step, full):
        mine = block(full, my_row)
        copies = [
            send(step, GATHER, m, mine, mine, (row_peer(2 * m), my_col)) for m in range(1, half)
        ]
        copies.append(send(step, GATHER, 0, mine, mine, (row_peer(1), my_col)))
        return copies

    def gather_finish(step, full, copies):
        passed = []
        for m in range(1, half):
            copies[m - 1].wait_recv()
            got = block(full, row_peer(2 * m))
            passed.append(send(step, GATHER, half + m, got, got, (row_peer(1), my_col)))
        copies[-1].wait_recv()
        for copy in passed:
            copy.wait_recv()

    def third_of():
        middle = near(identity - small_product(inverse_old, gram_old))
        return -small_product(
            small_product(near(square_old + gram_old), middle), inverse_older
        )

    gathers = gather_start(0, full_a)
    for i in range(stored):
        tile16[i] = entries_ref[i // slots, i % slots].astype(jnp.float32).astype(jnp.bfloat16)
    third = third_of()
    gather_finish(0, full_a, gathers)

    def forward(step, full):
        copies = []
        for r in range(tile_rows):
            total = None
            for s in range(slots):
                picked = full[cols_ref[r, s]]
                term = dot_t(digits(picked), tile16[r * slots + s])
                total = term if total is None else total + term
            partial[step, my_col, r] = fold_two(total[:order], total[order:])
            own = partial.at[step, my_col, r]
            for m in range(1, n_col):
                copies.append(
                    send(step, PARTIAL, r * n_col + m, own, own, (my_row, col_peer(m)))
                )
        return copies

    def summed_partial(step, r):
        total = partial[step, 0, r]
        for c in range(1, n_col):
            total = total + partial[step, c, r]
        return total

    sends = forward(0, full_a)
    for copy in sends:
        copy.wait_recv()
    projected = [near(summed_partial(0, r)) for r in range(tile_rows)]

    for step in range(2):
        gram_buf[step, my_row] = pack(gram_tiles(projected))
        own = gram_buf.at[step, my_row]
        grams = [send(step, GRAM, m, own, own, (row_peer(m), my_col)) for m in range(1, n_row)]

        for r in range(tile_rows):
            both = digits(projected[r])
            for s in range(slots):
                spread[r * slots + s] = dot(both, tile16[r * slots + s])
        total = jnp.zeros((2 * order, size), jnp.float32)
        running[0] = total
        for i in range(stored):
            total = total + spread[order_ref[i]]
            running[i + 1] = total
        scatters = []
        for m in range(n_row - 1, -1, -1):
            peer = row_peer(m)
            for t in range(share):
                tile = peer * share + t
                summed = running[end_ref[tile]] - running[begin_ref[tile]]
                outgoing[step, tile] = fold_two(summed[:order], summed[order:])
            if m:
                scatters.append(
                    send(
                        step, SCATTER, m, block(outgoing.at[step], peer),
                        incoming.at[step, m], (peer, my_col),
                    )
                )

        for copy in grams:
            copy.wait_recv()
        total = gram_buf[step, 0]
        for r in range(1, n_row):
            total = total + gram_buf[step, r]
        gram_now = unpack(near(total))
        inverse_now = inverse_of(gram_now)
        second = -small_product(gram_now, inverse_old)
        if step:
            third = third_of()
        parts = []
        for t in range(share):
            one = product_parts(second, earlier[t])
            two = product_parts(third, earliest[t])
            upper, mid, lower = [a + b for a, b in zip(one, two)]
            parts.append(near(upper) * 15.0 + near(mid) * 256.0 + lower)

        for copy in scatters:
            copy.wait_recv()
        applied = []
        for t in range(share):
            total = outgoing[step, my_row * share + t]
            for m in range(1, n_row):
                total = total + incoming[step, m, t]
            applied.append(near(total))

        ready = [near(applied[t] + parts[t]) for t in range(share)]
        if step == 0:
            for t in range(share):
                full_b[my_row * share + t] = ready[t]
            gathers = gather_start(1, full_b)

        square_row[step, my_row] = pack(gram_tiles(applied))
        own = square_row.at[step, my_row]
        squares = [
            send(step, SQUARE_ROW, m, own, own, (row_peer(m), my_col)) for m in range(1, n_row)
        ]
        if step == 0:
            gather_finish(1, full_b, gathers)
            sends = forward(1, full_b)
        for copy in squares:
            copy.wait_recv()
        total = square_row[step, 0]
        for r in range(1, n_row):
            total = total + square_row[step, r]
        square_col[step, my_col] = near(total)
        own = square_col.at[step, my_col]
        squares = [
            send(step, SQUARE_COL, m, own, own, (my_row, col_peer(m))) for m in range(1, n_col)
        ]
        for copy in squares:
            copy.wait_recv()
        total = square_col[step, 0]
        for c in range(1, n_col):
            total = total + square_col[step, c]
        square_now = unpack(near(total))

        first = near(identity - small_product(near(square_now + gram_now), inverse_now))
        if step == 0:
            rest = [fold_three(*product_parts(first, projected[r])) for r in range(tile_rows)]
            for copy in sends:
                copy.wait_recv()
            projected = [near(summed_partial(1, r) + rest[r]) for r in range(tile_rows)]
        following = []
        for t in range(share):
            upper, mid, lower = product_parts(first, current[t])
            following.append(
                whole(ready[t] + near(upper) * 15.0 + near(mid) * 256.0 + lower)
            )
        out = (next_ref, later_ref)[step]
        for t in range(share):
            out[:, t * size : (t + 1) * size] = following[t]
        earliest, earlier, current = earlier, current, [near(f) for f in following]
        inverse_older, inverse_old = inverse_old, inverse_now
        gram_old, square_old = gram_now, square_now

    for copy in started:
        copy.wait_send()


def body(
    n_row, n_col, entries, tile_cols, block_now, block_prev, block_prev2,
    gram_prev, square_prev, inverse_prev, inverse_prev2,
):
    tile_rows, slots, size = entries.shape[:3]
    order, width = block_now.shape
    share = width // size
    col_tiles = n_row * share
    stored = tile_rows * slots
    assert tile_rows <= 4 and share <= 4 and n_row % 2 == 0

    cols = tile_cols
    places = jnp.arange(tile_rows, dtype=jnp.int32)[:, None] * slots + jnp.arange(
        slots, dtype=jnp.int32
    )
    mine, other = cols[:, :, None, None], cols[None, None, :, :]
    ahead = (other < mine) | ((other == mine) & (places[None, None] < places[:, :, None, None]))
    rank = jnp.sum(ahead.astype(jnp.int32), axis=(2, 3))
    steps = jnp.arange(stored, dtype=jnp.int32)[:, None, None]
    ordered = jnp.sum(jnp.where(rank[None] == steps, places[None], 0), axis=(1, 2))
    tiles = jnp.arange(col_tiles, dtype=jnp.int32)[:, None, None]
    begin = jnp.sum((cols[None] < tiles).astype(jnp.int32), axis=(1, 2))
    end = jnp.sum((cols[None] <= tiles).astype(jnp.int32), axis=(1, 2))

    copies = max(n_row + 1, tile_rows * n_col)
    f32 = jnp.float32
    smem = pl.BlockSpec(memory_space=pltpu.SMEM)
    vmem = pl.BlockSpec(memory_space=pltpu.VMEM)
    packed = (order // 4, order * 4)
    following, later = pl.pallas_call(
        functools.partial(kernel, n_row, n_col),
        out_shape=(jax.ShapeDtypeStruct((order, width), f32),) * 2,
        in_specs=[smem] * 4 + [vmem] * 8,
        out_specs=(vmem, vmem),
        scratch_shapes=[
            pltpu.VMEM((stored, size, size), jnp.bfloat16),
            pltpu.VMEM((col_tiles, order, size), f32),
            pltpu.VMEM((col_tiles, order, size), f32),
            pltpu.VMEM((2, n_col, tile_rows, order, size), f32),
            pltpu.VMEM((stored, 2 * order, size), f32),
            pltpu.VMEM((stored + 1, 2 * order, size), f32),
            pltpu.VMEM((2, col_tiles, order, size), f32),
            pltpu.VMEM((2, n_row, share, order, size), f32),
            pltpu.VMEM((2, n_row) + packed, f32),
            pltpu.VMEM((2, n_row) + packed, f32),
            pltpu.VMEM((2, n_col) + packed, f32),
            pltpu.SemaphoreType.DMA((2, 6, copies)),
            pltpu.SemaphoreType.DMA((2, 6, copies)),
        ],
        compiler_params=pltpu.CompilerParams(collective_id=0, has_side_effects=True),
    )(
        cols, ordered, begin, end, entries, block_now, block_prev, block_prev2,
        gram_prev, square_prev, inverse_prev, inverse_prev2,
    )
    return following / modulus, later / modulus


def solution(mesh):
    placed = (
        P("row", "col", None, None),
        P("row", "col"),
        P(None, ("col", "row")),
        P(None, ("col", "row")),
        P(None, ("col", "row")),
        P(),
        P(),
        P(),
        P(),
    )
    return jax.shard_map(
        functools.partial(body, mesh.shape["row"], mesh.shape["col"]),
        mesh=mesh,
        in_specs=placed,
        out_specs=(P(None, ("col", "row")), P(None, ("col", "row"))),
        check_vma=False,
    )
```

```python
import functools

import jax
import jax.numpy as jnp
from jax import lax
from jax.experimental import pallas as pl
from jax.experimental.pallas import tpu as pltpu
from jax.sharding import PartitionSpec as P

modulus = 65521.0
reciprocal = 1.0 / 65521.0
MESH = pl.DeviceIdType.MESH
GATHER, PARTIAL, SCATTER, GRAM, SQUARE_ROW, SQUARE_COL = range(6)


def near(values):
    return values - jnp.floor(values * reciprocal + 0.5) * modulus


def whole(values):
    signed = near(values)
    return jnp.where(signed < 0.0, signed + modulus, signed)


def split(values):
    top = jnp.floor(values * (1.0 / 256.0) + 0.5)
    return top, values - top * 256.0


def digits(values):
    top, low = split(values)
    return jnp.concatenate([top, low], axis=0).astype(jnp.bfloat16)


def fold_two(top, low):
    return near(near(top) * 256.0 + low)


def fold_three(upper, middle, lower):
    return near(near(upper) * 15.0 + near(middle) * 256.0 + near(lower))


def mulmod(left, right):
    top, low = split(right)
    return near(near(left * top) * 256.0 + left * low)


def dot(left, right):
    return jnp.dot(left, right, preferred_element_type=jnp.float32)


def dot_t(left, right):
    return lax.dot_general(
        left, right, (((1,), (1,)), ((), ())), preferred_element_type=jnp.float32
    )


def product_parts(left, right):
    order = left.shape[0]
    left_digits = digits(left)
    right_top, right_low = split(right)
    with_top = dot(left_digits, right_top.astype(jnp.bfloat16))
    with_low = dot(left_digits, right_low.astype(jnp.bfloat16))
    return with_top[:order], with_top[order:] + with_low[:order], with_low[order:]


def small_product(left, right):
    return fold_three(*product_parts(left, right))


def gram_tiles(tiles):
    order = tiles[0].shape[0]
    total = None
    for tile in tiles:
        both = digits(tile)
        term = dot_t(both, both)
        total = term if total is None else total + term
    return fold_three(
        total[:order, :order],
        total[:order, order:] + total[order:, :order],
        total[order:, order:],
    )


def power_inverse(number):
    result = None
    square = number
    for position in range(16):
        if 65519 >> position & 1:
            result = square if result is None else mulmod(result, square)
        if position < 15:
            square = mulmod(square, square)
    return result


def identity_of(order):
    rows = lax.broadcasted_iota(jnp.int32, (order, order), 0)
    lanes = lax.broadcasted_iota(jnp.int32, (order, order), 1)
    return jnp.where(rows == lanes, 1.0, 0.0).astype(jnp.float32)


def inverse_of(matrix):
    order = matrix.shape[0]
    work = jnp.concatenate([matrix, identity_of(order)], axis=1)
    rows = lax.broadcasted_iota(jnp.int32, (order, 1), 0)
    for column in range(order):
        entry = work[:, column : column + 1]
        usable = (entry != 0.0) & (rows >= column)
        first = jnp.min(jnp.where(usable, rows, order), axis=0, keepdims=True)
        chosen = rows == jnp.where(first == order, column, first)
        pivot_row = jnp.sum(jnp.where(chosen, work, 0.0), axis=0, keepdims=True)
        pivot = jnp.sum(jnp.where(chosen, entry, 0.0), axis=0, keepdims=True)
        swapped = jnp.where(chosen, work[column : column + 1, :], work)
        factor = jnp.where(chosen, entry[column : column + 1, :], entry)
        pivot_row = jnp.where(pivot == 0.0, 0.0, pivot_row)
        pivot = jnp.where(pivot == 0.0, 1.0, pivot)
        pivot_top, pivot_low = split(pivot)
        factor_top, factor_low = split(factor)
        upper = near(pivot_top * swapped - factor_top * pivot_row)
        reduced = near(upper * 256.0 + (pivot_low * swapped - factor_low * pivot_row))
        work = jnp.where(rows == column, pivot_row, reduced)
    left = work[:, :order]
    diagonal = jnp.sum(left * identity_of(order), axis=1, keepdims=True)
    return mulmod(work[:, order:], power_inverse(diagonal))


def pack(values):
    rows = values.shape[0] // 4
    return jnp.concatenate([values[g * rows : (g + 1) * rows] for g in range(4)], axis=1)


def unpack(values):
    width = values.shape[1] // 4
    return jnp.concatenate([values[:, g * width : (g + 1) * width] for g in range(4)], axis=0)


def flipped(place, mask, count):
    assert count & (count - 1) == 0
    bit = 1
    moved = place
    while bit < count:
        if mask & bit:
            moved = moved + bit - 2 * bit * lax.rem(place // bit, 2)
        bit *= 2
    return moved


def kernel(
    n_row, n_col, cols_ref,
    entries_ref, now_ref, prev_ref, prev2_ref,
    gram_ref, square_ref, inverse_ref, inverse2_ref, next_ref, later_ref,
    tile16, full_a0, full_a1, full_b0, full_b1, partial, spread, running, outgoing, incoming,
    gram_buf, square_row, square_col, order_ref, begin_ref, send_sem, recv_sem,
):
    my_row = lax.axis_index("row")
    my_col = lax.axis_index("col")
    tile_rows, slots, size = entries_ref.shape[:3]
    stored = tile_rows * slots
    order = now_ref.shape[0]
    share = now_ref.shape[1] // size
    half = n_row // 2
    part = order // 2
    fulls = ((full_a0, full_a1), (full_b0, full_b1))
    started = []

    def row_peer(m):
        return flipped(my_row, m, n_row)

    def col_peer(m):
        return flipped(my_col, m, n_col)

    barrier = pltpu.get_barrier_semaphore()
    for m in range(1, n_row):
        pl.semaphore_signal(barrier, inc=1, device_id=(row_peer(m), my_col), device_id_type=MESH)
    for m in range(1, n_col):
        pl.semaphore_signal(barrier, inc=1, device_id=(my_row, col_peer(m)), device_id_type=MESH)

    def send(step, h, phase, k, source, target, device):
        copy = pltpu.make_async_remote_copy(
            src_ref=source, dst_ref=target,
            send_sem=send_sem.at[step, h, phase, k], recv_sem=recv_sem.at[step, h, phase, k],
            device_id=device, device_id_type=MESH,
        )
        copy.start()
        started.append(copy)
        return copy

    def tiles_of(values):
        return [values[:, t * size : (t + 1) * size] for t in range(share)]

    def load(ref):
        return tiles_of(near(ref[...].astype(jnp.float32)))

    def block(full, row):
        return full.at[pl.ds(row * share, share)]

    current, earlier, earliest = load(now_ref), load(prev_ref), load(prev2_ref)
    gram_old = near(gram_ref[...].astype(jnp.float32))
    square_old = near(square_ref[...].astype(jnp.float32))
    inverse_old = near(inverse_ref[...].astype(jnp.float32))
    inverse_older = near(inverse2_ref[...].astype(jnp.float32))
    identity = identity_of(order)

    def halves(values):
        return (values[:part], values[part:])

    def fill(step, tiles):
        for t in range(share):
            for h, rows in enumerate(halves(tiles[t])):
                fulls[step][h][my_row * share + t] = rows

    fill(0, current)
    pl.semaphore_wait(barrier, n_row + n_col - 2)

    def gather_start(step, h):
        mine = block(fulls[step][h], my_row)
        copies = [
            send(step, h, GATHER, m, mine, mine, (row_peer(2 * m), my_col))
            for m in range(1, half)
        ]
        copies.append(send(step, h, GATHER, 0, mine, mine, (row_peer(1), my_col)))
        return copies

    def gather_finish(step, h, copies):
        passed = []
        for m in range(1, half):
            copies[m - 1].wait_recv()
            got = block(fulls[step][h], row_peer(2 * m))
            passed.append(send(step, h, GATHER, half + m, got, got, (row_peer(1), my_col)))
        copies[-1].wait_recv()
        for copy in passed:
            copy.wait_recv()

    def third_of():
        middle = near(identity - small_product(inverse_old, gram_old))
        return -small_product(
            small_product(near(square_old + gram_old), middle), inverse_older
        )

    gathers = [gather_start(0, h) for h in range(2)]
    for i in range(stored):
        tile16[i] = entries_ref[i // slots, i % slots].astype(jnp.float32).astype(jnp.bfloat16)
    cols = [cols_ref[i // slots, i % slots] for i in range(stored)]

    def as_int(flag):
        return jnp.where(flag, 1, 0).astype(jnp.int32)

    ranks = []
    for i in range(stored):
        rank = jnp.int32(0)
        for j in range(stored):
            if j != i:
                rank = rank + as_int(cols[j] <= cols[i] if j < i else cols[j] < cols[i])
        ranks.append(rank)
    for k in range(stored):
        place = jnp.int32(0)
        for i in range(1, stored):
            place = place + jnp.where(ranks[i] == k, i, 0).astype(jnp.int32)
        order_ref[k] = place

    def count(tile, carry):
        below = jnp.int32(0)
        for i in range(stored):
            below = below + as_int(cols[i] < tile)
        begin_ref[tile] = below
        return carry

    lax.fori_loop(0, n_row * share + 1, count, 0)
    third = third_of()

    def forward(step, h):
        copies = []
        for r in range(tile_rows):
            total = None
            for s in range(slots):
                picked = fulls[step][h][cols[r * slots + s]]
                term = dot_t(digits(picked), tile16[r * slots + s])
                total = term if total is None else total + term
            partial[step, h, my_col, r] = fold_two(total[:part], total[part:])
            own = partial.at[step, h, my_col, r]
            for m in range(1, n_col):
                copies.append(
                    send(step, h, PARTIAL, r * n_col + m, own, own, (my_row, col_peer(m)))
                )
        return copies

    def summed_partial(step, h, r):
        total = partial[step, h, 0, r]
        for c in range(1, n_col):
            total = total + partial[step, h, c, r]
        return total

    sends = []
    for h in range(2):
        gather_finish(0, h, gathers[h])
        sends.append(forward(0, h))
    rest = None

    for step in range(2):
        pieces, scatters = [], []
        for h in range(2):
            for copy in sends[h]:
                copy.wait_recv()
            piece = []
            for r in range(tile_rows):
                total = summed_partial(step, h, r)
                piece.append(near(total if rest is None else total + halves(rest[r])[h]))
            pieces.append(piece)
            if h == 1:
                projected = [
                    jnp.concatenate([pieces[0][r], pieces[1][r]], axis=0) for r in range(tile_rows)
                ]
                gram_buf[step, my_row] = pack(gram_tiles(projected))
                own = gram_buf.at[step, my_row]
                grams = [
                    send(step, 0, GRAM, m, own, own, (row_peer(m), my_col))
                    for m in range(1, n_row)
                ]

            for r in range(tile_rows):
                both = digits(piece[r])
                for s in range(slots):
                    spread[r * slots + s] = dot(both, tile16[r * slots + s])
            total = jnp.zeros((order, size), jnp.float32)
            running[0] = total
            for i in range(stored):
                total = total + spread[order_ref[i]]
                running[i + 1] = total
            for m in range(n_row - 1, -1, -1):
                peer = row_peer(m)
                for t in range(share):
                    tile = peer * share + t
                    summed = running[begin_ref[tile + 1]] - running[begin_ref[tile]]
                    outgoing[step, h, tile] = fold_two(summed[:part], summed[part:])
                if m:
                    scatters.append(
                        send(
                            step, h, SCATTER, m, block(outgoing.at[step, h], peer),
                            incoming.at[step, h, m], (peer, my_col),
                        )
                    )

        for copy in grams:
            copy.wait_recv()
        total = gram_buf[step, 0]
        for r in range(1, n_row):
            total = total + gram_buf[step, r]
        gram_now = unpack(near(total))
        inverse_now = inverse_of(gram_now)
        second = -small_product(gram_now, inverse_old)
        if step:
            third = third_of()
        parts = []
        for t in range(share):
            one = product_parts(second, earlier[t])
            two = product_parts(third, earliest[t])
            upper, mid, lower = [a + b for a, b in zip(one, two)]
            parts.append(near(upper) * 15.0 + near(mid) * 256.0 + lower)

        for copy in scatters:
            copy.wait_recv()
        applied = []
        for t in range(share):
            rows = []
            for h in range(2):
                total = outgoing[step, h, my_row * share + t]
                for m in range(1, n_row):
                    total = total + incoming[step, h, m, t]
                rows.append(near(total))
            applied.append(jnp.concatenate(rows, axis=0))

        ready = [near(applied[t] + parts[t]) for t in range(share)]
        if step == 0:
            fill(1, ready)
            gathers = [gather_start(1, h) for h in range(2)]

        square_row[step, my_row] = pack(gram_tiles(applied))
        own = square_row.at[step, my_row]
        squares = [
            send(step, 0, SQUARE_ROW, m, own, own, (row_peer(m), my_col)) for m in range(1, n_row)
        ]
        if step == 0:
            gather_finish(1, 0, gathers[0])
            sends = [forward(1, 0)]
        for copy in squares:
            copy.wait_recv()
        total = square_row[step, 0]
        for r in range(1, n_row):
            total = total + square_row[step, r]
        square_col[step, my_col] = near(total)
        own = square_col.at[step, my_col]
        squares = [
            send(step, 0, SQUARE_COL, m, own, own, (my_row, col_peer(m))) for m in range(1, n_col)
        ]
        if step == 0:
            gather_finish(1, 1, gathers[1])
            sends.append(forward(1, 1))
        for copy in squares:
            copy.wait_recv()
        total = square_col[step, 0]
        for c in range(1, n_col):
            total = total + square_col[step, c]
        square_now = unpack(near(total))

        first = near(identity - small_product(near(square_now + gram_now), inverse_now))
        if step == 0:
            rest = [fold_three(*product_parts(first, projected[r])) for r in range(tile_rows)]
        following = []
        for t in range(share):
            upper, mid, lower = product_parts(first, current[t])
            following.append(
                whole(ready[t] + near(upper) * 15.0 + near(mid) * 256.0 + lower)
            )
        out = (next_ref, later_ref)[step]
        for t in range(share):
            out[:, t * size : (t + 1) * size] = following[t]
        earliest, earlier, current = earlier, current, [near(f) for f in following]
        inverse_older, inverse_old = inverse_old, inverse_now
        gram_old, square_old = gram_now, square_now

    for copy in started:
        copy.wait_send()


def body(
    n_row, n_col, entries, tile_cols, block_now, block_prev, block_prev2,
    gram_prev, square_prev, inverse_prev, inverse_prev2,
):
    tile_rows, slots, size = entries.shape[:3]
    order, width = block_now.shape
    share = width // size
    col_tiles = n_row * share
    stored = tile_rows * slots
    assert tile_rows <= 4 and share <= 4 and n_row % 2 == 0

    copies = max(n_row + 1, tile_rows * n_col)
    f32 = jnp.float32
    smem = pl.BlockSpec(memory_space=pltpu.SMEM)
    vmem = pl.BlockSpec(memory_space=pltpu.VMEM)
    packed = (order // 4, order * 4)
    part = order // 2
    following, later = pl.pallas_call(
        functools.partial(kernel, n_row, n_col),
        out_shape=(jax.ShapeDtypeStruct((order, width), f32),) * 2,
        in_specs=[smem] + [vmem] * 8,
        out_specs=(vmem, vmem),
        scratch_shapes=[
            pltpu.VMEM((stored, size, size), jnp.bfloat16),
            pltpu.VMEM((col_tiles, part, size), f32),
            pltpu.VMEM((col_tiles, part, size), f32),
            pltpu.VMEM((col_tiles, part, size), f32),
            pltpu.VMEM((col_tiles, part, size), f32),
            pltpu.VMEM((2, 2, n_col, tile_rows, part, size), f32),
            pltpu.VMEM((stored, order, size), f32),
            pltpu.VMEM((stored + 1, order, size), f32),
            pltpu.VMEM((2, 2, col_tiles, part, size), f32),
            pltpu.VMEM((2, 2, n_row, share, part, size), f32),
            pltpu.VMEM((2, n_row) + packed, f32),
            pltpu.VMEM((2, n_row) + packed, f32),
            pltpu.VMEM((2, n_col) + packed, f32),
            pltpu.SMEM((stored,), jnp.int32),
            pltpu.SMEM((col_tiles + 1,), jnp.int32),
            pltpu.SemaphoreType.DMA((2, 2, 6, copies)),
            pltpu.SemaphoreType.DMA((2, 2, 6, copies)),
        ],
        compiler_params=pltpu.CompilerParams(collective_id=0, has_side_effects=True),
    )(
        tile_cols, entries, block_now, block_prev, block_prev2,
        gram_prev, square_prev, inverse_prev, inverse_prev2,
    )
    return following / modulus, later / modulus


def solution(mesh):
    placed = (
        P("row", "col", None, None),
        P("row", "col"),
        P(None, ("col", "row")),
        P(None, ("col", "row")),
        P(None, ("col", "row")),
        P(),
        P(),
        P(),
        P(),
    )
    return jax.shard_map(
        functools.partial(body, mesh.shape["row"], mesh.shape["col"]),
        mesh=mesh,
        in_specs=placed,
        out_specs=(P(None, ("col", "row")), P(None, ("col", "row"))),
        check_vma=False,
    )
```

```python
import functools

import jax
import jax.numpy as jnp
from jax import lax
from jax.experimental import pallas as pl
from jax.experimental.pallas import tpu as pltpu
from jax.sharding import PartitionSpec as P

modulus = 65521.0
reciprocal = 1.0 / 65521.0
MESH = pl.DeviceIdType.MESH
GATHER, PARTIAL, SCATTER, GRAM, SQUARE_ROW, SQUARE_COL = range(6)


def near(values):
    return values - jnp.floor(values * reciprocal + 0.5) * modulus


def whole(values):
    signed = near(values)
    return jnp.where(signed < 0.0, signed + modulus, signed)


def split(values):
    top = jnp.floor(values * (1.0 / 256.0) + 0.5)
    return top, values - top * 256.0


def digits(values):
    top, low = split(values)
    return jnp.concatenate([top, low], axis=0).astype(jnp.bfloat16)


def fold_two(top, low):
    return near(near(top) * 256.0 + low)


def fold_three(upper, middle, lower):
    return near(near(upper) * 15.0 + near(middle) * 256.0 + near(lower))


def mulmod(left, right):
    top, low = split(right)
    return near(near(left * top) * 256.0 + left * low)


def dot(left, right):
    return jnp.dot(left, right, preferred_element_type=jnp.float32)


def dot_t(left, right):
    return lax.dot_general(
        left, right, (((1,), (1,)), ((), ())), preferred_element_type=jnp.float32
    )


def product_parts(left, right):
    order = left.shape[0]
    left_digits = digits(left)
    right_top, right_low = split(right)
    with_top = dot(left_digits, right_top.astype(jnp.bfloat16))
    with_low = dot(left_digits, right_low.astype(jnp.bfloat16))
    return with_top[:order], with_top[order:] + with_low[:order], with_low[order:]


def small_product(left, right):
    return fold_three(*product_parts(left, right))


def gram_tiles(tiles):
    order = tiles[0].shape[0]
    total = None
    for tile in tiles:
        both = digits(tile)
        term = dot_t(both, both)
        total = term if total is None else total + term
    return fold_three(
        total[:order, :order],
        total[:order, order:] + total[order:, :order],
        total[order:, order:],
    )


def power_inverse(number):
    result = None
    square = number
    for position in range(16):
        if 65519 >> position & 1:
            result = square if result is None else mulmod(result, square)
        if position < 15:
            square = mulmod(square, square)
    return result


def identity_of(order):
    rows = lax.broadcasted_iota(jnp.int32, (order, order), 0)
    lanes = lax.broadcasted_iota(jnp.int32, (order, order), 1)
    return jnp.where(rows == lanes, 1.0, 0.0).astype(jnp.float32)


def inverse_of(matrix):
    order = matrix.shape[0]
    work = jnp.concatenate([matrix, identity_of(order)], axis=1)
    rows = lax.broadcasted_iota(jnp.int32, (order, 1), 0)
    for column in range(order):
        entry = work[:, column : column + 1]
        usable = (entry != 0.0) & (rows >= column)
        first = jnp.min(jnp.where(usable, rows, order), axis=0, keepdims=True)
        chosen = rows == jnp.where(first == order, column, first)
        pivot_row = jnp.sum(jnp.where(chosen, work, 0.0), axis=0, keepdims=True)
        pivot = jnp.sum(jnp.where(chosen, entry, 0.0), axis=0, keepdims=True)
        swapped = jnp.where(chosen, work[column : column + 1, :], work)
        factor = jnp.where(chosen, entry[column : column + 1, :], entry)
        pivot_row = jnp.where(pivot == 0.0, 0.0, pivot_row)
        pivot = jnp.where(pivot == 0.0, 1.0, pivot)
        pivot_top, pivot_low = split(pivot)
        factor_top, factor_low = split(factor)
        upper = near(pivot_top * swapped - factor_top * pivot_row)
        reduced = near(upper * 256.0 + (pivot_low * swapped - factor_low * pivot_row))
        work = jnp.where(rows == column, pivot_row, reduced)
    left = work[:, :order]
    diagonal = jnp.sum(left * identity_of(order), axis=1, keepdims=True)
    return mulmod(work[:, order:], power_inverse(diagonal))


def pack(values):
    rows = values.shape[0] // 4
    return jnp.concatenate([values[g * rows : (g + 1) * rows] for g in range(4)], axis=1)


def unpack(values):
    width = values.shape[1] // 4
    return jnp.concatenate([values[:, g * width : (g + 1) * width] for g in range(4)], axis=0)


def flipped(place, mask, count):
    assert count & (count - 1) == 0
    bit = 1
    moved = place
    while bit < count:
        if mask & bit:
            moved = moved + bit - 2 * bit * lax.rem(place // bit, 2)
        bit *= 2
    return moved


def kernel(
    n_row, n_col, cols_ref,
    entries_ref, now_ref, prev_ref, prev2_ref,
    gram_ref, square_ref, inverse_ref, inverse2_ref, next_ref, later_ref,
    tile16, full_a, full_b, partial, spread, running, outgoing, incoming,
    gram_buf, square_row, square_col, order_ref, begin_ref, send_sem, recv_sem,
):
    my_row = lax.axis_index("row")
    my_col = lax.axis_index("col")
    tile_rows, slots, size = entries_ref.shape[:3]
    stored = tile_rows * slots
    order = now_ref.shape[0]
    share = now_ref.shape[1] // size
    half = n_row // 2
    started = []

    def row_peer(m):
        return flipped(my_row, m, n_row)

    def col_peer(m):
        return flipped(my_col, m, n_col)

    barrier = pltpu.get_barrier_semaphore()
    for m in range(1, n_row):
        pl.semaphore_signal(barrier, inc=1, device_id=(row_peer(m), my_col), device_id_type=MESH)
    for m in range(1, n_col):
        pl.semaphore_signal(barrier, inc=1, device_id=(my_row, col_peer(m)), device_id_type=MESH)

    def send(step, phase, k, source, target, device):
        copy = pltpu.make_async_remote_copy(
            src_ref=source, dst_ref=target,
            send_sem=send_sem.at[step, phase, k], recv_sem=recv_sem.at[step, phase, k],
            device_id=device, device_id_type=MESH,
        )
        copy.start()
        started.append(copy)
        return copy

    def tiles_of(values):
        return [values[:, t * size : (t + 1) * size] for t in range(share)]

    def load(ref):
        return tiles_of(near(ref[...].astype(jnp.float32)))

    def block(full, row):
        return full.at[pl.ds(row * share, share)]

    current, earlier, earliest = load(now_ref), load(prev_ref), load(prev2_ref)
    gram_old = near(gram_ref[...].astype(jnp.float32))
    square_old = near(square_ref[...].astype(jnp.float32))
    inverse_old = near(inverse_ref[...].astype(jnp.float32))
    inverse_older = near(inverse2_ref[...].astype(jnp.float32))
    identity = identity_of(order)
    for t in range(share):
        full_a[my_row * share + t] = current[t]
    pl.semaphore_wait(barrier, n_row + n_col - 2)

    def gather_start(step, full):
        mine = block(full, my_row)
        copies = [
            send(step, GATHER, m, mine, mine, (row_peer(2 * m), my_col)) for m in range(1, half)
        ]
        copies.append(send(step, GATHER, 0, mine, mine, (row_peer(1), my_col)))
        return copies

    def gather_finish(step, full, copies):
        passed = []
        for m in range(1, half):
            copies[m - 1].wait_recv()
            got = block(full, row_peer(2 * m))
            passed.append(send(step, GATHER, half + m, got, got, (row_peer(1), my_col)))
        copies[-1].wait_recv()
        for copy in passed:
            copy.wait_recv()

    def third_of():
        middle = near(identity - small_product(inverse_old, gram_old))
        return -small_product(
            small_product(near(square_old + gram_old), middle), inverse_older
        )

    gathers = gather_start(0, full_a)
    for i in range(stored):
        tile16[i] = entries_ref[i // slots, i % slots].astype(jnp.float32).astype(jnp.bfloat16)
    cols = [cols_ref[i // slots, i % slots] for i in range(stored)]

    def as_int(flag):
        return jnp.where(flag, 1, 0).astype(jnp.int32)

    ranks = []
    for i in range(stored):
        rank = jnp.int32(0)
        for j in range(stored):
            if j != i:
                rank = rank + as_int(cols[j] <= cols[i] if j < i else cols[j] < cols[i])
        ranks.append(rank)
    for k in range(stored):
        place = jnp.int32(0)
        for i in range(1, stored):
            place = place + jnp.where(ranks[i] == k, i, 0).astype(jnp.int32)
        order_ref[k] = place

    def count(tile, carry):
        below = jnp.int32(0)
        for i in range(stored):
            below = below + as_int(cols[i] < tile)
        begin_ref[tile] = below
        return carry

    lax.fori_loop(0, n_row * share + 1, count, 0)
    third = third_of()
    gather_finish(0, full_a, gathers)

    def forward(step, full):
        copies = []
        for r in range(tile_rows):
            total = None
            for s in range(slots):
                picked = full[cols[r * slots + s]]
                term = dot_t(digits(picked), tile16[r * slots + s])
                total = term if total is None else total + term
            partial[step, my_col, r] = fold_two(total[:order], total[order:])
            own = partial.at[step, my_col, r]
            for m in range(1, n_col):
                copies.append(
                    send(step, PARTIAL, r * n_col + m, own, own, (my_row, col_peer(m)))
                )
        return copies

    def summed_partial(step, r):
        total = partial[step, 0, r]
        for c in range(1, n_col):
            total = total + partial[step, c, r]
        return total

    sends = forward(0, full_a)
    for copy in sends:
        copy.wait_recv()
    projected = [near(summed_partial(0, r)) for r in range(tile_rows)]

    for step in range(2):
        gram_buf[step, my_row] = pack(gram_tiles(projected))
        own = gram_buf.at[step, my_row]
        grams = [send(step, GRAM, m, own, own, (row_peer(m), my_col)) for m in range(1, n_row)]

        for r in range(tile_rows):
            both = digits(projected[r])
            for s in range(slots):
                spread[r * slots + s] = dot(both, tile16[r * slots + s])
        total = jnp.zeros((2 * order, size), jnp.float32)
        running[0] = total
        for i in range(stored):
            total = total + spread[order_ref[i]]
            running[i + 1] = total
        scatters = []
        for m in range(n_row - 1, -1, -1):
            peer = row_peer(m)
            for t in range(share):
                tile = peer * share + t
                summed = running[begin_ref[tile + 1]] - running[begin_ref[tile]]
                outgoing[step, tile] = fold_two(summed[:order], summed[order:])
            if m:
                scatters.append(
                    send(
                        step, SCATTER, m, block(outgoing.at[step], peer),
                        incoming.at[step, m], (peer, my_col),
                    )
                )

        for copy in grams:
            copy.wait_recv()
        total = gram_buf[step, 0]
        for r in range(1, n_row):
            total = total + gram_buf[step, r]
        gram_now = unpack(near(total))
        inverse_now = inverse_of(gram_now)
        second = -small_product(gram_now, inverse_old)
        if step:
            third = third_of()
        parts = []
        for t in range(share):
            one = product_parts(second, earlier[t])
            two = product_parts(third, earliest[t])
            upper, mid, lower = [a + b for a, b in zip(one, two)]
            parts.append(near(upper) * 15.0 + near(mid) * 256.0 + lower)

        for copy in scatters:
            copy.wait_recv()
        applied = []
        for t in range(share):
            total = outgoing[step, my_row * share + t]
            for m in range(1, n_row):
                total = total + incoming[step, m, t]
            applied.append(near(total))

        ready = [near(applied[t] + parts[t]) for t in range(share)]
        if step == 0:
            for t in range(share):
                full_b[my_row * share + t] = ready[t]
            gathers = gather_start(1, full_b)

        square_row[step, my_row] = pack(gram_tiles(applied))
        own = square_row.at[step, my_row]
        squares = [
            send(step, SQUARE_ROW, m, own, own, (row_peer(m), my_col)) for m in range(1, n_row)
        ]
        if step == 0:
            gather_finish(1, full_b, gathers)
            sends = forward(1, full_b)
        for copy in squares:
            copy.wait_recv()
        total = square_row[step, 0]
        for r in range(1, n_row):
            total = total + square_row[step, r]
        square_col[step, my_col] = near(total)
        own = square_col.at[step, my_col]
        squares = [
            send(step, SQUARE_COL, m, own, own, (my_row, col_peer(m))) for m in range(1, n_col)
        ]
        for copy in squares:
            copy.wait_recv()
        total = square_col[step, 0]
        for c in range(1, n_col):
            total = total + square_col[step, c]
        square_now = unpack(near(total))

        first = near(identity - small_product(near(square_now + gram_now), inverse_now))
        if step == 0:
            rest = [fold_three(*product_parts(first, projected[r])) for r in range(tile_rows)]
            for copy in sends:
                copy.wait_recv()
            projected = [near(summed_partial(1, r) + rest[r]) for r in range(tile_rows)]
        following = []
        for t in range(share):
            upper, mid, lower = product_parts(first, current[t])
            following.append(
                whole(ready[t] + near(upper) * 15.0 + near(mid) * 256.0 + lower)
            )
        out = (next_ref, later_ref)[step]
        for t in range(share):
            out[:, t * size : (t + 1) * size] = following[t]
        earliest, earlier, current = earlier, current, [near(f) for f in following]
        inverse_older, inverse_old = inverse_old, inverse_now
        gram_old, square_old = gram_now, square_now

    for copy in started:
        copy.wait_send()


def body(
    n_row, n_col, entries, tile_cols, block_now, block_prev, block_prev2,
    gram_prev, square_prev, inverse_prev, inverse_prev2,
):
    tile_rows, slots, size = entries.shape[:3]
    order, width = block_now.shape
    share = width // size
    col_tiles = n_row * share
    stored = tile_rows * slots
    assert tile_rows <= 4 and share <= 4 and n_row % 2 == 0

    copies = max(n_row + 1, tile_rows * n_col)
    f32 = jnp.float32
    smem = pl.BlockSpec(memory_space=pltpu.SMEM)
    vmem = pl.BlockSpec(memory_space=pltpu.VMEM)
    packed = (order // 4, order * 4)
    following, later = pl.pallas_call(
        functools.partial(kernel, n_row, n_col),
        out_shape=(jax.ShapeDtypeStruct((order, width), f32),) * 2,
        in_specs=[smem] + [vmem] * 8,
        out_specs=(vmem, vmem),
        scratch_shapes=[
            pltpu.VMEM((stored, size, size), jnp.bfloat16),
            pltpu.VMEM((col_tiles, order, size), f32),
            pltpu.VMEM((col_tiles, order, size), f32),
            pltpu.VMEM((2, n_col, tile_rows, order, size), f32),
            pltpu.VMEM((stored, 2 * order, size), f32),
            pltpu.VMEM((stored + 1, 2 * order, size), f32),
            pltpu.VMEM((2, col_tiles, order, size), f32),
            pltpu.VMEM((2, n_row, share, order, size), f32),
            pltpu.VMEM((2, n_row) + packed, f32),
            pltpu.VMEM((2, n_row) + packed, f32),
            pltpu.VMEM((2, n_col) + packed, f32),
            pltpu.SMEM((stored,), jnp.int32),
            pltpu.SMEM((col_tiles + 1,), jnp.int32),
            pltpu.SemaphoreType.DMA((2, 6, copies)),
            pltpu.SemaphoreType.DMA((2, 6, copies)),
        ],
        compiler_params=pltpu.CompilerParams(collective_id=0, has_side_effects=True),
    )(
        tile_cols, entries, block_now, block_prev, block_prev2,
        gram_prev, square_prev, inverse_prev, inverse_prev2,
    )
    return following / modulus, later / modulus


def solution(mesh):
    placed = (
        P("row", "col", None, None),
        P("row", "col"),
        P(None, ("col", "row")),
        P(None, ("col", "row")),
        P(None, ("col", "row")),
        P(),
        P(),
        P(),
        P(),
    )
    return jax.shard_map(
        functools.partial(body, mesh.shape["row"], mesh.shape["col"]),
        mesh=mesh,
        in_specs=placed,
        out_specs=(P(None, ("col", "row")), P(None, ("col", "row"))),
        check_vma=False,
    )
```

```python
import functools

import jax
import jax.numpy as jnp
from jax import lax
from jax.experimental import pallas as pl
from jax.experimental.pallas import tpu as pltpu
from jax.sharding import PartitionSpec as P

modulus = 65521.0
reciprocal = 1.0 / 65521.0
MESH = pl.DeviceIdType.MESH
GATHER, PARTIAL, SCATTER, GRAM, SQUARE_ROW, SQUARE_COL = range(6)


def near(values):
    return values - jnp.floor(values * reciprocal + 0.5) * modulus


def whole(values):
    signed = near(values)
    return jnp.where(signed < 0.0, signed + modulus, signed)


def split(values):
    top = jnp.floor(values * (1.0 / 256.0) + 0.5)
    return top, values - top * 256.0


def digits(values):
    top, low = split(values)
    return jnp.concatenate([top, low], axis=0).astype(jnp.bfloat16)


def fold_two(top, low):
    return near(near(top) * 256.0 + low)


def fold_three(upper, middle, lower):
    return near(near(upper) * 15.0 + near(middle) * 256.0 + near(lower))


def mulmod(left, right):
    top, low = split(right)
    return near(near(left * top) * 256.0 + left * low)


def dot(left, right):
    return jnp.dot(left, right, preferred_element_type=jnp.float32)


def dot_t(left, right):
    return lax.dot_general(
        left, right, (((1,), (1,)), ((), ())), preferred_element_type=jnp.float32
    )


def product_parts(left, right):
    order = left.shape[0]
    left_digits = digits(left)
    right_top, right_low = split(right)
    with_top = dot(left_digits, right_top.astype(jnp.bfloat16))
    with_low = dot(left_digits, right_low.astype(jnp.bfloat16))
    return with_top[:order], with_top[order:] + with_low[:order], with_low[order:]


def small_product(left, right):
    return fold_three(*product_parts(left, right))


def gram_tiles(tiles):
    order = tiles[0].shape[0]
    total = None
    for tile in tiles:
        both = digits(tile)
        term = dot_t(both, both)
        total = term if total is None else total + term
    return fold_three(
        total[:order, :order],
        total[:order, order:] + total[order:, :order],
        total[order:, order:],
    )


def power_inverse(number):
    result = None
    square = number
    for position in range(16):
        if 65519 >> position & 1:
            result = square if result is None else mulmod(result, square)
        if position < 15:
            square = mulmod(square, square)
    return result


def identity_of(order):
    rows = lax.broadcasted_iota(jnp.int32, (order, order), 0)
    lanes = lax.broadcasted_iota(jnp.int32, (order, order), 1)
    return jnp.where(rows == lanes, 1.0, 0.0).astype(jnp.float32)


def inverse_of(matrix):
    order = matrix.shape[0]
    work = jnp.concatenate([matrix, identity_of(order)], axis=1)
    rows = lax.broadcasted_iota(jnp.int32, (order, 1), 0)
    for column in range(order):
        entry = work[:, column : column + 1]
        usable = (entry != 0.0) & (rows >= column)
        first = jnp.min(jnp.where(usable, rows, order), axis=0, keepdims=True)
        chosen = rows == jnp.where(first == order, column, first)
        pivot_row = jnp.sum(jnp.where(chosen, work, 0.0), axis=0, keepdims=True)
        pivot = jnp.sum(jnp.where(chosen, entry, 0.0), axis=0, keepdims=True)
        swapped = jnp.where(chosen, work[column : column + 1, :], work)
        factor = jnp.where(chosen, entry[column : column + 1, :], entry)
        pivot_row = jnp.where(pivot == 0.0, 0.0, pivot_row)
        pivot = jnp.where(pivot == 0.0, 1.0, pivot)
        pivot_top, pivot_low = split(pivot)
        factor_top, factor_low = split(factor)
        upper = near(pivot_top * swapped - factor_top * pivot_row)
        reduced = near(upper * 256.0 + (pivot_low * swapped - factor_low * pivot_row))
        work = jnp.where(rows == column, pivot_row, reduced)
    left = work[:, :order]
    diagonal = jnp.sum(left * identity_of(order), axis=1, keepdims=True)
    return mulmod(work[:, order:], power_inverse(diagonal))


def pack(values):
    rows = values.shape[0] // 4
    return jnp.concatenate([values[g * rows : (g + 1) * rows] for g in range(4)], axis=1)


def unpack(values):
    width = values.shape[1] // 4
    return jnp.concatenate([values[:, g * width : (g + 1) * width] for g in range(4)], axis=0)


def flipped(place, mask, count):
    assert count & (count - 1) == 0
    bit = 1
    moved = place
    while bit < count:
        if mask & bit:
            moved = moved + bit - 2 * bit * lax.rem(place // bit, 2)
        bit *= 2
    return moved


def kernel(
    n_row, n_col, cols_ref,
    entries_ref, now_ref, prev_ref, prev2_ref,
    gram_ref, square_ref, inverse_ref, inverse2_ref, next_ref, later_ref,
    tile16, full_a, full_b, partial, spread, running, outgoing, incoming,
    gram_buf, square_row, square_col, order_ref, begin_ref, send_sem, recv_sem,
):
    my_row = lax.axis_index("row")
    my_col = lax.axis_index("col")
    tile_rows, slots, size = entries_ref.shape[:3]
    stored = tile_rows * slots
    order = now_ref.shape[0]
    share = now_ref.shape[1] // size
    half = n_row // 2
    started = []

    def row_peer(m):
        return flipped(my_row, m, n_row)

    def col_peer(m):
        return flipped(my_col, m, n_col)

    barrier = pltpu.get_barrier_semaphore()
    for m in range(1, n_row):
        pl.semaphore_signal(barrier, inc=1, device_id=(row_peer(m), my_col), device_id_type=MESH)
    for m in range(1, n_col):
        pl.semaphore_signal(barrier, inc=1, device_id=(my_row, col_peer(m)), device_id_type=MESH)

    def send(step, phase, k, source, target, device):
        copy = pltpu.make_async_remote_copy(
            src_ref=source, dst_ref=target,
            send_sem=send_sem.at[step, phase, k], recv_sem=recv_sem.at[step, phase, k],
            device_id=device, device_id_type=MESH,
        )
        copy.start()
        started.append(copy)
        return copy

    def tiles_of(values):
        return [values[:, t * size : (t + 1) * size] for t in range(share)]

    def load(ref):
        return tiles_of(near(ref[...].astype(jnp.float32)))

    def block(full, row):
        return full.at[pl.ds(row * share, share)]

    current, earlier, earliest = load(now_ref), load(prev_ref), load(prev2_ref)
    gram_old = near(gram_ref[...].astype(jnp.float32))
    square_old = near(square_ref[...].astype(jnp.float32))
    inverse_old = near(inverse_ref[...].astype(jnp.float32))
    inverse_older = near(inverse2_ref[...].astype(jnp.float32))
    identity = identity_of(order)
    for t in range(share):
        full_a[my_row * share + t] = current[t]
    pl.semaphore_wait(barrier, n_row + n_col - 2)

    def gather_start(step, full):
        mine = block(full, my_row)
        copies = [
            send(step, GATHER, m, mine, mine, (row_peer(2 * m), my_col)) for m in range(1, half)
        ]
        copies.append(send(step, GATHER, 0, mine, mine, (row_peer(1), my_col)))
        return copies

    def gather_finish(step, full, copies):
        passed = []
        for m in range(1, half):
            copies[m - 1].wait_recv()
            got = block(full, row_peer(2 * m))
            passed.append(send(step, GATHER, half + m, got, got, (row_peer(1), my_col)))
        copies[-1].wait_recv()
        for copy in passed:
            copy.wait_recv()

    def third_of():
        middle = near(identity - small_product(inverse_old, gram_old))
        return -small_product(
            small_product(near(square_old + gram_old), middle), inverse_older
        )

    gathers = gather_start(0, full_a)
    for i in range(stored):
        tile16[i] = entries_ref[i // slots, i % slots].astype(jnp.float32).astype(jnp.bfloat16)
    cols = [cols_ref[i // slots, i % slots] for i in range(stored)]

    def as_int(flag):
        return jnp.where(flag, 1, 0).astype(jnp.int32)

    ranks = []
    for i in range(stored):
        rank = jnp.int32(0)
        for j in range(stored):
            if j != i:
                rank = rank + as_int(cols[j] <= cols[i] if j < i else cols[j] < cols[i])
        ranks.append(rank)
    for k in range(stored):
        place = jnp.int32(0)
        for i in range(1, stored):
            place = place + jnp.where(ranks[i] == k, i, 0).astype(jnp.int32)
        order_ref[k] = place

    def count(tile, carry):
        below = jnp.int32(0)
        for i in range(stored):
            below = below + as_int(cols[i] < tile)
        begin_ref[tile] = below
        return carry

    lax.fori_loop(0, n_row * share + 1, count, 0)
    third = third_of()
    gather_finish(0, full_a, gathers)

    def forward(step, full):
        copies = []
        for r in range(tile_rows):
            total = None
            for s in range(slots):
                picked = full[cols[r * slots + s]]
                term = dot_t(digits(picked), tile16[r * slots + s])
                total = term if total is None else total + term
            partial[step, my_col, r] = fold_two(total[:order], total[order:])
            own = partial.at[step, my_col, r]
            for m in range(1, n_col):
                copies.append(
                    send(step, PARTIAL, r * n_col + m, own, own, (my_row, col_peer(m)))
                )
        return copies

    def summed_partial(step, r):
        total = partial[step, 0, r]
        for c in range(1, n_col):
            total = total + partial[step, c, r]
        return total

    sends = forward(0, full_a)
    for copy in sends:
        copy.wait_recv()
    projected = [near(summed_partial(0, r)) for r in range(tile_rows)]

    for step in range(2):
        gram_buf[step, my_row] = pack(gram_tiles(projected))
        own = gram_buf.at[step, my_row]
        grams = [send(step, GRAM, m, own, own, (row_peer(m), my_col)) for m in range(1, n_row)]

        for r in range(tile_rows):
            both = digits(projected[r])
            for s in range(slots):
                spread[r * slots + s] = dot(both, tile16[r * slots + s])
        total = jnp.zeros((2 * order, size), jnp.float32)
        running[0] = total
        for i in range(stored):
            total = total + spread[order_ref[i]]
            running[i + 1] = total
        def finish_block(peer):
            for t in range(share):
                tile = peer * share + t
                summed = running[begin_ref[tile + 1]] - running[begin_ref[tile]]
                outgoing[step, tile] = fold_two(summed[:order], summed[order:])

        across = {}
        for m in range(half - 1, -1, -1):
            peer = row_peer(2 * m + 1)
            finish_block(peer)
            across[m] = send(
                step, SCATTER, m, block(outgoing.at[step], peer),
                incoming.at[step, m], (row_peer(1), my_col),
            )
        for m in range(half - 1, -1, -1):
            finish_block(row_peer(2 * m))
        scatters = []
        for m in range(half - 1, 0, -1):
            across[m].wait_recv()
            peer = row_peer(2 * m)
            for t in range(share):
                outgoing[step, peer * share + t] = (
                    outgoing[step, peer * share + t] + incoming[step, m, t]
                )
            scatters.append(
                send(
                    step, SCATTER, half + m, block(outgoing.at[step], peer),
                    incoming.at[step, half + m], (peer, my_col),
                )
            )
        scatters.append(across[0])

        for copy in grams:
            copy.wait_recv()
        total = gram_buf[step, 0]
        for r in range(1, n_row):
            total = total + gram_buf[step, r]
        gram_now = unpack(near(total))
        inverse_now = inverse_of(gram_now)
        second = -small_product(gram_now, inverse_old)
        if step:
            third = third_of()
        parts = []
        for t in range(share):
            one = product_parts(second, earlier[t])
            two = product_parts(third, earliest[t])
            upper, mid, lower = [a + b for a, b in zip(one, two)]
            parts.append(near(upper) * 15.0 + near(mid) * 256.0 + lower)

        for copy in scatters:
            copy.wait_recv()
        applied = []
        for t in range(share):
            total = outgoing[step, my_row * share + t]
            for m in [0] + list(range(half + 1, n_row)):
                total = total + incoming[step, m, t]
            applied.append(near(total))

        ready = [near(applied[t] + parts[t]) for t in range(share)]
        if step == 0:
            for t in range(share):
                full_b[my_row * share + t] = ready[t]
            gathers = gather_start(1, full_b)

        square_row[step, my_row] = pack(gram_tiles(applied))
        own = square_row.at[step, my_row]
        squares = [
            send(step, SQUARE_ROW, m, own, own, (row_peer(m), my_col)) for m in range(1, n_row)
        ]
        if step == 0:
            gather_finish(1, full_b, gathers)
            sends = forward(1, full_b)
        for copy in squares:
            copy.wait_recv()
        total = square_row[step, 0]
        for r in range(1, n_row):
            total = total + square_row[step, r]
        square_col[step, my_col] = near(total)
        own = square_col.at[step, my_col]
        squares = [
            send(step, SQUARE_COL, m, own, own, (my_row, col_peer(m))) for m in range(1, n_col)
        ]
        for copy in squares:
            copy.wait_recv()
        total = square_col[step, 0]
        for c in range(1, n_col):
            total = total + square_col[step, c]
        square_now = unpack(near(total))

        first = near(identity - small_product(near(square_now + gram_now), inverse_now))
        if step == 0:
            rest = [fold_three(*product_parts(first, projected[r])) for r in range(tile_rows)]
            for copy in sends:
                copy.wait_recv()
            projected = [near(summed_partial(1, r) + rest[r]) for r in range(tile_rows)]
        following = []
        for t in range(share):
            upper, mid, lower = product_parts(first, current[t])
            following.append(
                whole(ready[t] + near(upper) * 15.0 + near(mid) * 256.0 + lower)
            )
        out = (next_ref, later_ref)[step]
        for t in range(share):
            out[:, t * size : (t + 1) * size] = following[t]
        earliest, earlier, current = earlier, current, [near(f) for f in following]
        inverse_older, inverse_old = inverse_old, inverse_now
        gram_old, square_old = gram_now, square_now

    for copy in started:
        copy.wait_send()


def body(
    n_row, n_col, entries, tile_cols, block_now, block_prev, block_prev2,
    gram_prev, square_prev, inverse_prev, inverse_prev2,
):
    tile_rows, slots, size = entries.shape[:3]
    order, width = block_now.shape
    share = width // size
    col_tiles = n_row * share
    stored = tile_rows * slots
    assert tile_rows <= 4 and share <= 4 and n_row % 2 == 0

    copies = max(n_row + 1, tile_rows * n_col)
    f32 = jnp.float32
    smem = pl.BlockSpec(memory_space=pltpu.SMEM)
    vmem = pl.BlockSpec(memory_space=pltpu.VMEM)
    packed = (order // 4, order * 4)
    following, later = pl.pallas_call(
        functools.partial(kernel, n_row, n_col),
        out_shape=(jax.ShapeDtypeStruct((order, width), f32),) * 2,
        in_specs=[smem] + [vmem] * 8,
        out_specs=(vmem, vmem),
        scratch_shapes=[
            pltpu.VMEM((stored, size, size), jnp.bfloat16),
            pltpu.VMEM((col_tiles, order, size), f32),
            pltpu.VMEM((col_tiles, order, size), f32),
            pltpu.VMEM((2, n_col, tile_rows, order, size), f32),
            pltpu.VMEM((stored, 2 * order, size), f32),
            pltpu.VMEM((stored + 1, 2 * order, size), f32),
            pltpu.VMEM((2, col_tiles, order, size), f32),
            pltpu.VMEM((2, n_row, share, order, size), f32),
            pltpu.VMEM((2, n_row) + packed, f32),
            pltpu.VMEM((2, n_row) + packed, f32),
            pltpu.VMEM((2, n_col) + packed, f32),
            pltpu.SMEM((stored,), jnp.int32),
            pltpu.SMEM((col_tiles + 1,), jnp.int32),
            pltpu.SemaphoreType.DMA((2, 6, copies)),
            pltpu.SemaphoreType.DMA((2, 6, copies)),
        ],
        compiler_params=pltpu.CompilerParams(collective_id=0, has_side_effects=True),
    )(
        tile_cols, entries, block_now, block_prev, block_prev2,
        gram_prev, square_prev, inverse_prev, inverse_prev2,
    )
    return following / modulus, later / modulus


def solution(mesh):
    placed = (
        P("row", "col", None, None),
        P("row", "col"),
        P(None, ("col", "row")),
        P(None, ("col", "row")),
        P(None, ("col", "row")),
        P(),
        P(),
        P(),
        P(),
    )
    return jax.shard_map(
        functools.partial(body, mesh.shape["row"], mesh.shape["col"]),
        mesh=mesh,
        in_specs=placed,
        out_specs=(P(None, ("col", "row")), P(None, ("col", "row"))),
        check_vma=False,
    )
```
